32 devices in a mesh: groups: 2 (over x), gy: 16 (over z, y, core).
Axes of the slice: x: 2, y: 2, z: 4, core: 2. Of those that a mesh axis runs over, the one named last changes fastest.
Arguments:
- tiles: bfloat16 [1024, 16, 128], P(('groups', 'gy')), parts along dimension 0, may hold values from -6 to 6
- entry_dest: int32 [1024, 1], P('groups'), parts along dimension 0, may hold values from 0 to 15; in each aligned block of 32 rows (0 to 31, 32 to 63, ...) at most 4 rows name the same one
- entry_tile: int32 [1024], P('groups'), parts along dimension 0, may hold values from 0 to 31
- entry_z: int32 [1024], P('groups'), parts along dimension 0, may hold values from 0 to 3
- entry_xb: int32 [1024], P('groups'), parts along dimension 0, may hold values from 0 to 3
- entry_ky: int32 [1024], P('groups'), parts along dimension 0, may hold values from 0 to 7
- entry_kx: int32 [1024], P('groups'), parts along dimension 0, may hold values from 0 to 7
- wy_table: bfloat16 [8, 8, 16], replicated, may hold values from 0 to 1
- wx_table: bfloat16 [8, 128, 128], replicated, may hold values from 0 to 1
- w_first: bfloat16 [32, 1, 3, 3, 3], replicated, may hold values from -1.25 to 1.25
- b_first: float32 [32], replicated, may hold values from -1.5 to 1.5
- w_second: bfloat16 [32, 32, 3, 3, 3], replicated, may hold values from -0.21875 to 0.21875
- b_second: float32 [32], replicated, may hold values from -1.5 to 1.5
- w_third: bfloat16 [32, 32, 3, 3, 3], replicated, may hold values from -0.21875 to 0.21875
- b_third: float32 [32], replicated, may hold values from -1.5 to 1.5
Outputs:
- affinity_features: bfloat16 [32, 8, 128, 512], P(None, 'groups', 'gy'), parts along dimension 1
The draws below stay inside these ranges and needn't reach their ends.
There are 2 independent parts, one for each index of `groups`. The reference program is written for one: setup_inputs(seed, part) draws one part's arguments, and reference() takes and returns one part's arrays. A program takes and returns all parts, laid end to end along the dimension named above; an argument that names none is the same for every part. Nothing has to cross between parts.
Inputs may be any that keep to these rules, and one draw needn't show every extreme that they name: `entry_dest`: rows 32 * s to 32 * s + 31 are the entries of the tiles of device s of gy; among one device's rows no brick is named more than 4 times, a bound that some block reaches.
All inputs are finite; a program needn't handle non-finite values.
Results may differ from the reference program's by a relative error of at most 0.0064.
Values may be sent and summed in bfloat16 or wider, within the bound.
A program may use at most 64 MiB of HBM per device.

```python
import math
import jax
import jax.numpy as jnp
import numpy as np
from jax import lax

C = 32
X = 512
YB = 8
Z = 4
SH = 16
SW = 128
TILES_DEV = 32
CAP = 4
KY = 8
KX = 8
E_DEV = 32
ENTRIES = 512
N_GY = 16


def draw_wy_table(key, part):
    fraction = jax.random.uniform(key, (KY, YB, 1), jnp.float32)
    out_row = lax.broadcasted_iota(jnp.int32, (KY, YB, SH), 1)
    source_row = lax.broadcasted_iota(jnp.int32, (KY, YB, SH), 2)
    lower_row = out_row * SH // YB
    upper_row = jnp.minimum(lower_row + 1, SH - 1)
    low_weight = jnp.where(source_row == lower_row, 1.0 - fraction, 0.0)
    high_weight = jnp.where(source_row == upper_row, fraction, 0.0)
    return (low_weight + high_weight).astype(jnp.bfloat16)


def draw_wx_table(key, part):
    fraction = jax.random.uniform(key, (KX, 1, SW), jnp.float32)
    source_col = lax.broadcasted_iota(jnp.int32, (KX, SW, SW), 1)
    output_col = lax.broadcasted_iota(jnp.int32, (KX, SW, SW), 2)
    upper_col = jnp.minimum(output_col + 1, SW - 1)
    low_weight = jnp.where(source_col == output_col, 1.0 - fraction, 0.0)
    high_weight = jnp.where(source_col == upper_col, fraction, 0.0)
    return (low_weight + high_weight).astype(jnp.bfloat16)


def with_ends(drawn, key, smallest, top_value):
    shape = drawn.shape
    place = [jax.random.randint(jax.random.fold_in(key, axis), (), 0, shape[axis]) for axis in range(len(shape))]
    drawn = drawn.at[tuple(place)].set(smallest)
    longest = shape.index(max(shape))
    place[longest] = (place[longest] + 1) % shape[longest]
    return drawn.at[tuple(place)].set(top_value)


def block_scale(stream_key, dims, pieces, low, top_value):
    factor_of, own = 1.0, jax.random.fold_in(stream_key, 6)
    for axis_at, shards_of in pieces:
        steps = jnp.exp(jax.random.uniform(jax.random.fold_in(own, axis_at), (shards_of,), jnp.float32, low / len(pieces), top_value / len(pieces)))
        factor_of = factor_of * jnp.repeat(steps, dims[axis_at] // shards_of).reshape([-1 if axis == axis_at else 1 for axis in range(len(dims))])
    return factor_of


def assign_block(rng, own, number, rows, count, top, most, slope):
    ranking = jax.random.permutation(rng, count)
    crowded, usual = shares(count, rows * top, most, slope, True), shares(count, rows * top, most, slope, False)
    places = jnp.arange(count)

    def named(tallies, turn):
        used = int((tallies > 0).sum())
        fixed = max(1, used // 4)
        passed = fixed + (places - fixed + turn * (used - fixed)) % max(1, count - fixed)
        return jnp.zeros((count,), jnp.int32).at[ranking[jnp.where(places < fixed, places, passed)]].set(jnp.asarray(tallies, jnp.int32))

    tallies = jnp.where(number % 4 == 0, named(crowded, number // 4), named(usual, number - number // 4 - 1))
    mixed = jax.random.permutation(jax.random.fold_in(own, 3), count)
    donor, receiver = mixed[0:count // 2 * 2:2], mixed[1:count // 2 * 2:2]
    slack = jnp.minimum(tallies[donor] - 1, most - tallies[receiver]) // 2
    slack = jnp.where((donor == ranking[0]) | (receiver == ranking[0]) | (tallies[receiver] == 0), 0, jnp.maximum(slack, 0))
    passed = jax.random.randint(jax.random.fold_in(own, 4), (count // 2,), 0, 1 << 20) % (slack + 1)
    tallies = tallies.at[donor].add(-passed).at[receiver].add(passed)
    members = jnp.searchsorted(jnp.cumsum(tallies), jnp.arange(rows * top), side="right").astype(jnp.int32)
    listing = members.reshape(top, rows).T
    listing = listing[jax.random.permutation(jax.random.fold_in(own, 1), rows)]
    turn = jax.random.randint(jax.random.fold_in(own, 2), (rows, 1), 0, top)
    return jnp.take_along_axis(listing, (jnp.arange(top)[None, :] + turn) % top, axis=1)


def shares(count, total, most, slope, full):
    loads = [(1 << 20) // math.isqrt(standing ** slope) + 1 for standing in range(1, count + 1)]
    largest = most if full else min(most, max(-(-total // count), total * loads[0] // sum(loads)))
    least = 1 if total - largest >= count - 1 else 0
    counts, surplus = [largest] + [least] * (count - 1), total - largest - least * (count - 1)
    while surplus > 0:
        candidates = [i for i in range(1, count) if counts[i] < largest] or [i for i in range(1, count) if counts[i] < most]
        mass, left = sum([loads[i] for i in candidates]), surplus
        for i in candidates:
            addition = min(most - counts[i], max(1, left * loads[i] // mass), surplus)
            counts[i] = counts[i] + addition
            surplus = surplus - addition
    return np.array(counts)


def centred(key, shape, scale, most, shards=(), kind=jnp.bfloat16):
    drawn = jax.random.normal(key, shape, jnp.float32) * scale
    if len(shards) > 0:
        drawn = block_scale(key, shape, shards, -0.22, 0.18) * drawn
    return jnp.clip(drawn, min=-most, max=most).astype(kind)


def setup_inputs(seed: int = 0, part: int = 0) -> dict:
    keys = jax.random.split(jax.random.key(seed), 16)
    part_keys = jax.random.split(jax.random.fold_in(keys[15], part), 16)
    tiles = centred(part_keys[0], (N_GY * TILES_DEV, SH, SW), 1.0, 6.0, ((0, 16),))
    entry_dest_keys = jax.random.split(jax.random.fold_in(part_keys[1], 1), ENTRIES // E_DEV)
    entry_dest_turns = jax.random.permutation(jax.random.fold_in(part_keys[1], 3), ENTRIES // E_DEV)
    entry_dest = jax.vmap(lambda own, number: assign_block(jax.random.fold_in(part_keys[1], 2), own, number, E_DEV, N_GY, 1, CAP, 2))(entry_dest_keys, entry_dest_turns).reshape((ENTRIES, 1))
    entry_tile = with_ends(jax.random.randint(part_keys[2], (ENTRIES,), 0, TILES_DEV), jax.random.fold_in(part_keys[2], 1), 0, TILES_DEV - 1).astype(jnp.int32)
    entry_z = with_ends(jax.random.randint(part_keys[3], (ENTRIES,), 0, Z), jax.random.fold_in(part_keys[3], 1), 0, Z - 1).astype(jnp.int32)
    entry_xb = with_ends(jax.random.randint(part_keys[4], (ENTRIES,), 0, X // SW), jax.random.fold_in(part_keys[4], 1), 0, (X // SW) - 1).astype(jnp.int32)
    entry_ky = with_ends(jax.random.randint(part_keys[5], (ENTRIES,), 0, KY), jax.random.fold_in(part_keys[5], 1), 0, KY - 1).astype(jnp.int32)
    entry_kx = with_ends(jax.random.randint(part_keys[6], (ENTRIES,), 0, KX), jax.random.fold_in(part_keys[6], 1), 0, KX - 1).astype(jnp.int32)
    wy_table = draw_wy_table(jax.random.fold_in(keys[15], 71), part)
    wx_table = draw_wx_table(jax.random.fold_in(keys[15], 71), part)
    w_first = centred(keys[9], (C, 1, 3, 3, 3), 27 ** -0.5, 1.25)
    b_first = centred(keys[10], (C,), 0.3, 1.5, (), jnp.float32)
    w_second = centred(keys[11], (C, C, 3, 3, 3), (27 * C) ** -0.5, 0.21875)
    b_second = centred(keys[12], (C,), 0.3, 1.5, (), jnp.float32)
    w_third = centred(keys[13], (C, C, 3, 3, 3), (27 * C) ** -0.5, 0.21875)
    b_third = centred(keys[14], (C,), 0.3, 1.5, (), jnp.float32)
    return dict(tiles=tiles, entry_dest=entry_dest, entry_tile=entry_tile, entry_z=entry_z, entry_xb=entry_xb, entry_ky=entry_ky, entry_kx=entry_kx, wy_table=wy_table, wx_table=wx_table, w_first=w_first, b_first=b_first, w_second=w_second, b_second=b_second, w_third=w_third, b_third=b_third)


def conv_layer(features, weight, bias):
    result = lax.conv_general_dilated(
        features[None].astype(jnp.float32), weight.astype(jnp.float32), (1, 1, 1),
        ((1, 1), (1, 1), (1, 1)), dimension_numbers=("NCDHW", "OIDHW", "NCDHW"),
        precision=lax.Precision.HIGHEST)[0]
    return jax.nn.relu(result + bias[:, None, None, None]).astype(jnp.bfloat16)


def reference(tiles, entry_dest, entry_tile, entry_z, entry_xb, entry_ky, entry_kx, wy_table, wx_table, w_first, b_first, w_second, b_second, w_third, b_third):
    target_brick = entry_dest[:, 0]
    count = target_brick.shape[0]
    per_device = count // N_GY
    source = (jnp.arange(count, dtype=jnp.int32) // per_device).astype(jnp.int32)
    picked = tiles[(source * TILES_DEV + entry_tile).astype(jnp.int32)].astype(jnp.float32)
    vertical = wy_table[entry_ky].astype(jnp.float32)
    row_samples = jnp.einsum("eys,esw->eyw", vertical, picked).astype(jnp.bfloat16)
    flat_rows = row_samples.reshape(count * YB, SW)
    patches = jnp.zeros((count, YB, SW), jnp.float32)
    for block_index in range(KX):
        product = jnp.dot(flat_rows, wx_table[block_index], preferred_element_type=jnp.float32).reshape(count, YB, SW)
        patches = patches + jnp.where((entry_kx == block_index)[:, None, None], product, jnp.zeros_like(product))
    rendered = jnp.zeros((Z, N_GY, YB, X // SW, SW), jnp.float32)
    rendered = rendered.at[entry_z, target_brick, :, entry_xb, :].add(patches)
    image = rendered.reshape(Z, N_GY * YB, X).astype(jnp.bfloat16)
    first = conv_layer(image[None], w_first, b_first)
    second = conv_layer(first, w_second, b_second)
    return conv_layer(second, w_third, b_third)
```

```python
import jax
import jax.numpy as jnp
import numpy as np
from jax import lax
from jax.experimental import pallas as pl
from jax.experimental.pallas import tpu as pltpu
from jax.sharding import PartitionSpec as P

X = 512
YB = 8
Z = 4
CAP = 4


def with_halo(cells, sides, width):
    for axis, dim in sides:
        count = lax.axis_size(axis)
        ends = count - 1
        head = lax.slice_in_dim(cells, 0, width, axis=dim)
        tail = lax.slice_in_dim(cells, cells.shape[dim] - width, cells.shape[dim], axis=dim)
        cells = jnp.concatenate(
            [
                lax.ppermute(tail, axis, [(i, (i + 1) % count) for i in range(ends)]),
                cells,
                lax.ppermute(head, axis, [((i + 1) % count, i) for i in range(ends)]),
            ],
            axis=dim,
        )
    return cells


def first_taps():
    taps = np.zeros((27, 2, Z, 3, 4, Z), np.float32)
    for yo in range(2):
        for zo in range(Z):
            for c in range(3):
                for b in range(3):
                    for a in range(3):
                        zi = zo + a - 1
                        if 0 <= zi < Z:
                            taps[(a * 3 + b) * 3 + c, yo, zo, c, yo + b, zi] = 1.0
    return taps.reshape(27, 2 * Z, 12 * Z)


def shifted(value):
    lane = lax.broadcasted_iota(jnp.int32, value.shape, 1)
    width = value.shape[1]
    before = jnp.where(lane == 0, 0.0, pltpu.roll(value, 1, 1))
    after = jnp.where(lane == width - 1, 0.0, pltpu.roll(value, width - 1, 1))
    return before, value, after


def convolutions(image_ref, taps_ref, band_ref, bias_ref, out_ref, band, first, second, third):
    own_index = lax.axis_index("gy")
    last_index = lax.axis_size("gy") - 1
    channels = out_ref.shape[0]
    plane = Z * channels
    lane = lax.broadcasted_iota(jnp.int32, (band_ref.shape[1], plane), 1)
    band[...] = jnp.zeros_like(band)
    for layer in range(2):
        source = band_ref[layer].astype(jnp.float32)
        for zo in range(Z):
            offset = (zo - 1) * channels
            placed = source if offset == 0 else pltpu.roll(source, offset % plane, 1)
            placed = jnp.where((lane >= offset) & (lane < offset + 3 * channels), placed, 0.0)
            placed = placed.astype(jnp.bfloat16)
            for c in range(3):
                for b in range(3):
                    block = placed[(c * 3 + b) * channels : (c * 3 + b + 1) * channels]
                    for yo in range(2):
                        rows = (yo * Z + zo) * channels
                        cols = ((yo + b) * 3 + c) * plane
                        band[layer, rows : rows + channels, cols : cols + plane] = block

    def keep(result, target, pair, pairs, extra_rows):
        result = jnp.maximum(result, 0.0)
        for yo in range(2):
            row = 2 * pair + yo - extra_rows
            part = result[yo * plane : (yo + 1) * plane]
            if row < 0:
                part = jnp.where(own_index > 0, part, 0.0)
            if row >= YB:
                part = jnp.where(own_index < last_index, part, 0.0)
            for c, moved in enumerate(shifted(part)):
                start = ((2 * pair + yo) * 3 + c) * plane
                target[start : start + plane, :] = moved.astype(jnp.bfloat16)

    pieces = shifted(image_ref[...].astype(jnp.float32))
    pairs = YB // 2 + 2
    for pair in range(pairs):
        window = jnp.concatenate(
            [
                piece[2 * pair * Z : (2 * pair + 4) * Z].astype(jnp.bfloat16)
                for piece in pieces
            ],
            axis=0,
        )
        result = jnp.dot(taps_ref[...], window, preferred_element_type=jnp.float32)
        keep(result + bias_ref[:, 0:1], first, pair, pairs, 2)
    depth = 12 * plane
    for pair in range(YB // 2 + 1):
        window = first[6 * pair * plane : 6 * pair * plane + depth, :]
        result = jnp.dot(band[0], window, preferred_element_type=jnp.float32)
        keep(result + bias_ref[:, 1:2], second, pair, YB // 2 + 1, 1)
    for pair in range(YB // 2):
        window = second[6 * pair * plane : 6 * pair * plane + depth, :]
        result = jnp.dot(band[1], window, preferred_element_type=jnp.float32)
        result = jnp.maximum(result + bias_ref[:, 2:3], 0.0)
        for yo in range(2):
            for zo in range(Z):
                rows = (yo * Z + zo) * channels
                start = zo * YB + 2 * pair + yo
                for block in range(third.shape[0]):
                    third[block, pl.ds(start, channels, stride=Z * YB), :] = result[
                        rows : rows + channels, block * 128 : (block + 1) * 128
                    ]
    for block in range(third.shape[0]):
        out_ref[:, :, :, block * 128 : (block + 1) * 128] = (
            third[block].reshape(channels, Z, YB, 128).astype(jnp.bfloat16)
        )


def network(image, w_first, b_first, w_second, b_second, w_third, b_third):
    channels = w_first.shape[0]
    width = image.shape[1]
    plane = Z * channels
    taps = jnp.einsum(
        "ot,trk->rok",
        w_first.reshape(channels, 27),
        first_taps().astype(jnp.bfloat16),
        preferred_element_type=jnp.float32,
    )
    taps = taps.astype(jnp.bfloat16).reshape(2 * plane, 12 * Z)
    weights = jnp.stack([w_second, w_third]).transpose(0, 5, 4, 1, 3, 2)
    weights = jnp.pad(weights, ((0, 0), (0, 0), (0, 0), (0, 0), (0, 1), (0, 0)))
    weights = weights.reshape(2, 9 * channels, 4 * channels)
    biases = jnp.tile(jnp.stack([b_first, b_second, b_third], axis=1), (2 * Z, 1))
    vmem = pl.BlockSpec(memory_space=pltpu.VMEM)
    return pl.pallas_call(
        convolutions,
        out_shape=jax.ShapeDtypeStruct((channels, Z, YB, width), jnp.bfloat16),
        in_specs=[vmem] * 4,
        out_specs=vmem,
        scratch_shapes=[
            pltpu.VMEM((2, 2 * plane, 12 * plane), jnp.bfloat16),
            pltpu.VMEM((3 * plane * (YB + 4), width), jnp.bfloat16),
            pltpu.VMEM((3 * plane * (YB + 2), width), jnp.bfloat16),
            pltpu.VMEM((width // 128, plane * YB, 128), jnp.float32),
        ],
        compiler_params=pltpu.CompilerParams(vmem_limit_bytes=48 << 20),
        name="network",
    )(image, taps, weights, biases)


def on_device(
    tiles,
    entry_dest,
    entry_tile,
    entry_z,
    entry_xb,
    entry_ky,
    entry_kx,
    wy_table,
    wx_table,
    w_first,
    b_first,
    w_second,
    b_second,
    w_third,
    b_third,
):
    devices_gy = lax.axis_size("gy")
    own_index = lax.axis_index("gy")
    tiles_dev, tile_rows, tile_cols = tiles.shape
    per_device = entry_dest.shape[0] // devices_gy
    slot_total = devices_gy * CAP
    target_brick = entry_dest[:, 0].reshape(devices_gy, per_device)
    later_pos = lax.broadcasted_iota(jnp.int32, (per_device, per_device), 0)
    earlier_pos = lax.broadcasted_iota(jnp.int32, (per_device, per_device), 1)
    same_brick = (target_brick[:, :, None] == target_brick[:, None, :]) & (earlier_pos < later_pos)[
        None
    ]
    slot_rank = jnp.sum(same_brick, axis=2, dtype=jnp.int32)
    capacity_iota = lax.broadcasted_iota(jnp.int32, (1, CAP, 1), 1)
    matched = (
        (target_brick == own_index)[:, None, :] & (slot_rank[:, None, :] == capacity_iota)
    ).astype(jnp.float32)
    slot_live = jnp.sum(matched, axis=2).reshape(-1) > 0.5

    def slot_field(field):
        return (
            jnp.sum(matched * field.reshape(devices_gy, 1, per_device).astype(jnp.float32), axis=2)
            .reshape(-1)
            .astype(jnp.int32)
        )

    slot_z = slot_field(entry_z)
    slot_xb = slot_field(entry_xb)
    slot_ky = slot_field(entry_ky)
    slot_kx = slot_field(entry_kx)
    local_tiles = tiles.reshape(tiles_dev, tile_rows * tile_cols)
    own_brick = lax.dynamic_index_in_dim(target_brick, own_index, 0, keepdims=False)
    own_rank = lax.dynamic_index_in_dim(slot_rank, own_index, 0, keepdims=False)
    own_tile = lax.dynamic_index_in_dim(
        entry_tile.reshape(devices_gy, per_device), own_index, 0, keepdims=False
    )
    slot_target = own_brick * CAP + own_rank
    chooser = (
        lax.broadcasted_iota(jnp.int32, (slot_total, per_device), 0) == slot_target[None, :]
    ).astype(jnp.bfloat16)
    tile_choice = (
        own_tile[:, None] == lax.broadcasted_iota(jnp.int32, (per_device, tiles_dev), 1)
    ).astype(jnp.bfloat16)
    pick_matrix = jnp.dot(chooser, tile_choice, preferred_element_type=jnp.float32).astype(
        jnp.bfloat16
    )
    send_buffer = jnp.dot(pick_matrix, local_tiles, preferred_element_type=jnp.float32).astype(
        jnp.bfloat16
    )
    send_buffer = send_buffer.reshape(devices_gy, CAP, tile_rows * tile_cols)
    arrived = lax.all_to_all(send_buffer, "gy", split_axis=0, concat_axis=0, tiled=True).reshape(
        slot_total, tile_rows, tile_cols
    )
    ky_onehot = (
        slot_ky[:, None] == lax.broadcasted_iota(jnp.int32, (1, wy_table.shape[0]), 1)
    ).astype(jnp.bfloat16)
    vertical = jnp.einsum(
        "mk,kys->mys", ky_onehot, wy_table, preferred_element_type=jnp.float32
    ).astype(jnp.bfloat16)
    row_samples = jnp.einsum(
        "mys,msw->myw", vertical, arrived, preferred_element_type=jnp.float32
    ).astype(jnp.bfloat16)
    kx_onehot = (
        slot_kx[:, None] == lax.broadcasted_iota(jnp.int32, (1, wx_table.shape[0]), 1)
    ).astype(jnp.bfloat16)
    horizontal = jnp.einsum(
        "mk,ksp->msp", kx_onehot, wx_table, preferred_element_type=jnp.float32
    ).astype(jnp.bfloat16)
    patches = jnp.einsum(
        "myw,mwp->myp", row_samples, horizontal, preferred_element_type=jnp.float32
    )
    x_blocks = X // tile_cols
    placement = (
        (slot_z * x_blocks + slot_xb)[:, None]
        == lax.broadcasted_iota(jnp.int32, (1, Z * x_blocks), 1)
    ) & slot_live[:, None]
    rendered = jnp.einsum(
        "mq,myp->qyp", placement.astype(jnp.float32), patches, precision=lax.Precision.HIGHEST
    )
    image = (
        rendered.reshape(Z, x_blocks, YB, tile_cols)
        .transpose(0, 2, 1, 3)
        .reshape(Z, YB, X)
        .astype(jnp.bfloat16)
    )
    extended = with_halo(image[None], (("gy", 2),), 3)
    rows = extended[0].transpose(1, 0, 2).reshape((YB + 6) * Z, X)
    return network(rows, w_first, b_first, w_second, b_second, w_third, b_third)


def solution(mesh):
    return jax.shard_map(
        on_device,
        mesh=mesh,
        in_specs=(
            P(("groups", "gy"), None, None),
            P("groups", None),
            P("groups"),
            P("groups"),
            P("groups"),
            P("groups"),
            P("groups"),
            P(),
            P(),
            P(),
            P(),
            P(),
            P(),
            P(),
            P(),
        ),
        out_specs=P(None, "groups", "gy", None),
        check_vma=False,
    )
```

```python
import jax
import jax.numpy as jnp
import numpy as np
from jax import lax
from jax.experimental import pallas as pl
from jax.experimental.pallas import tpu as pltpu
from jax.sharding import PartitionSpec as P

X = 512
YB = 8
Z = 4
CAP = 4
HALO = 3


MESH = pl.DeviceIdType.MESH
GROUP = 4
NT = (((1,), (1,)), ((), ()))


def message_row(line):
    own, before = line < CAP * YB, line < CAP * (YB + HALO)
    side = jnp.where(before, line - CAP * YB, line - CAP * (YB + HALO))
    offset = jnp.where(own, 0, jnp.where(before, -1, 1))
    slot = jnp.where(own, line // YB, side // HALO)
    rest = jnp.where(own, line % YB, side % HALO)
    row = jnp.where(own | ~before, rest, rest + YB - HALO)
    used = line < CAP * (YB + 2 * HALO)
    return jnp.where(used, offset * CAP + slot, -1000), row, row + offset * YB + HALO


def iota(shape, axis):
    return lax.broadcasted_iota(jnp.int32, shape, axis)


def onehot(mask):
    return jnp.where(mask, 1.0, 0.0).astype(jnp.bfloat16)


def render(
    tiles_ref, dest_ref, tile_ref, z_ref, xb_ref, ky_ref, kx_ref, wy_ref, wx_ref, image_ref,
    fields, sent, arrived, send_sem, recv_sem,
):
    count = lax.axis_size("gy")
    own_index = lax.axis_index("gy")
    lines = sent.shape[1]
    live = CAP * (YB + 2 * HALO)
    lanes = dest_ref.shape[1]
    per_device = dest_ref.shape[0] * lanes // count
    window = YB + 2 * HALO
    order = sorted(range(1, count), key=lambda i: -min(i, count - i))

    arrived[:, live - live % 16 :, :] = jnp.zeros(
        (count, lines - live + live % 16, arrived.shape[2]), jnp.bfloat16
    )
    barrier = pltpu.get_barrier_semaphore()
    for i in order:
        pl.semaphore_signal(
            barrier, inc=1, device_id={"gy": lax.rem(own_index + i, count)}, device_id_type=MESH
        )

    dest = dest_ref[...]
    place = iota(dest.shape, 1) % per_device
    rank = jnp.zeros_like(dest)
    for step in range(1, per_device):
        same = (pltpu.roll(dest, step, 1) == dest) & (place >= step)
        rank = rank + jnp.where(same, 1, 0)
    rows = [
        dest * CAP + rank,
        ky_ref[...],
        tile_ref[...],
        kx_ref[...] + 1,
        xb_ref[...] * (window * Z) + z_ref[...] + 1,
    ]
    rows = [row.astype(jnp.float32) for row in rows]
    rows = rows + [jnp.zeros_like(rows[0])] * 3
    span = GROUP * per_device // lanes
    for group in range(count // GROUP):
        for part in range(span):
            line = group * span + part
            fields[group, :, part * lanes : (part + 1) * lanes] = jnp.concatenate(
                [row[line : line + 1] for row in rows], axis=0
            )

    own_group = own_index // GROUP
    mine = fields[own_group].astype(jnp.bfloat16)
    samples = per_device * YB
    expand = onehot(
        iota((samples, GROUP * per_device), 1)
        == iota((samples, GROUP * per_device), 0) // YB + (own_index % GROUP) * per_device
    )
    column = lax.dot_general(expand, mine, NT, preferred_element_type=jnp.float32)
    along = lax.dot_general(mine, expand, NT, preferred_element_type=jnp.float32)
    blocks, tile_rows = wy_ref.shape
    spot = iota((samples, blocks), 1)
    picked = onehot(
        ((spot // YB).astype(jnp.float32) == column[:, 1:2])
        & (spot % YB == iota((samples, blocks), 0) % YB)
    )
    vertical = jnp.dot(picked, wy_ref[...], preferred_element_type=jnp.float32)
    pixels = tiles_ref.shape[0]
    repeat = onehot(iota((tile_rows, pixels), 1) % tile_rows == iota((tile_rows, pixels), 0))
    vertical = jnp.dot(
        vertical.astype(jnp.bfloat16), repeat, preferred_element_type=jnp.float32
    )
    chosen = (iota((samples, pixels), 1) // tile_rows).astype(jnp.float32) == column[:, 2:3]
    vertical = jnp.where(chosen, vertical, 0.0).astype(jnp.bfloat16)
    row_samples = jnp.dot(
        vertical, tiles_ref[...], preferred_element_type=jnp.float32
    ).astype(jnp.bfloat16)

    key, row, _ = message_row(iota((lines, samples), 0))
    wanted = along[0:1, :] - key.astype(jnp.float32)
    wanted = jnp.where(row == iota((lines, samples), 1) % YB, wanted, -4000.0)

    def message(number):
        target = lax.rem(own_index + number, count)
        return onehot(wanted == (target * CAP).astype(jnp.float32))

    copies = []
    order = order + [0]
    for start in range(0, count, GROUP):
        numbers = order[start : start + GROUP]
        packed = jnp.dot(
            jnp.concatenate([message(number) for number in numbers], axis=0),
            row_samples,
            preferred_element_type=jnp.float32,
        ).astype(jnp.bfloat16)
        for part, number in enumerate(numbers):
            block = packed[part * lines : (part + 1) * lines]
            if number == 0:
                arrived[own_index] = block
            else:
                sent[number] = block
        if start == 0:
            pl.semaphore_wait(barrier, count - 1)
        for number in numbers:
            if number > 0:
                copy = pltpu.make_async_remote_copy(
                    src_ref=sent.at[number, 0:live],
                    dst_ref=arrived.at[own_index, 0:live],
                    send_sem=send_sem.at[number],
                    recv_sem=recv_sem.at[number],
                    device_id={"gy": lax.rem(own_index + number, count)},
                    device_id_type=MESH,
                )
                copy.start()
                copies.append(copy)

    depth = GROUP * lines
    entries = GROUP * per_device
    total = None
    horizontals = wx_ref.shape[0] // wx_ref.shape[1]
    key, _, window_row = message_row(iota((depth, entries), 0) % lines)
    sources = iota((depth, entries), 0) // lines == iota((depth, entries), 1) // per_device
    wanted_key = jnp.where(sources, key + own_index * CAP, -5000).astype(jnp.float32)
    _, _, target_row = message_row(iota((1, depth), 1) % lines)
    x_blocks = image_ref.shape[1] // wx_ref.shape[1]
    targets = x_blocks * window * Z
    meta = []
    for group in range(count // GROUP):
        held = fields[group]
        match = onehot(held[0:1, :] == wanted_key)
        held = held.astype(jnp.bfloat16)
        source = lax.dot_general(match, held, NT, preferred_element_type=jnp.float32)
        target = lax.dot_general(held, match, NT, preferred_element_type=jnp.float32)
        code = target[4:5, :]
        code = jnp.where(
            code > 0.5, code - 1.0 + (target_row * Z).astype(jnp.float32), -1.0
        )
        placed = onehot(iota((targets, depth), 0).astype(jnp.float32) == code)
        meta.append((source[:, 3:4], placed))
    for copy in copies:
        copy.wait()
    for group in range(count // GROUP):
        horizontal, placed = meta[group]
        samples_in = jnp.concatenate(
            [arrived[group * GROUP + part] for part in range(GROUP)], axis=0
        ).astype(jnp.float32)
        spread = jnp.concatenate(
            [
                jnp.where(horizontal == float(block + 1), samples_in, 0.0).astype(jnp.bfloat16)
                for block in range(horizontals)
            ],
            axis=1,
        )
        patches = jnp.dot(spread, wx_ref[...], preferred_element_type=jnp.float32)
        high = patches.astype(jnp.bfloat16)
        rest = patches - high.astype(jnp.float32)
        middle = rest.astype(jnp.bfloat16)
        low = (rest - middle.astype(jnp.float32)).astype(jnp.bfloat16)
        part = jnp.dot(
            placed, jnp.concatenate([high, middle, low], axis=1), preferred_element_type=jnp.float32
        )
        total = part if total is None else total + part
    columns = wx_ref.shape[1]
    total = total[:, :columns] + total[:, columns : 2 * columns] + total[:, 2 * columns :]
    for block in range(x_blocks):
        image_ref[:, block * columns : (block + 1) * columns] = total[
            block * window * Z : (block + 1) * window * Z
        ].astype(jnp.bfloat16)


def rendered_window(tiles, entries, wy_table, wx_table):
    count = lax.axis_size("gy")
    tiles_dev, tile_rows, tile_cols = tiles.shape
    lines = -(-CAP * (YB + 2 * HALO) // 16) * 16
    per_device = entries[0].size // count
    entries = [entry.reshape(-1, 128) for entry in entries]
    vmem = pl.BlockSpec(memory_space=pltpu.VMEM)
    return pl.pallas_call(
        render,
        out_shape=jax.ShapeDtypeStruct(((YB + 2 * HALO) * Z, X), jnp.bfloat16),
        in_specs=[vmem] * 9,
        out_specs=vmem,
        scratch_shapes=[
            pltpu.VMEM((count // GROUP, 8, GROUP * per_device), jnp.float32),
            pltpu.VMEM((count, lines, tile_cols), jnp.bfloat16),
            pltpu.VMEM((count, lines, tile_cols), jnp.bfloat16),
            pltpu.SemaphoreType.DMA((count,)),
            pltpu.SemaphoreType.DMA((count,)),
        ],
        compiler_params=pltpu.CompilerParams(
            collective_id=0, has_side_effects=True, vmem_limit_bytes=48 << 20
        ),
        name="render",
    )(
        tiles.reshape(tiles_dev * tile_rows, tile_cols),
        *entries,
        wy_table.reshape(-1, tile_rows),
        wx_table.reshape(-1, tile_cols),
    )


def first_taps():
    taps = np.zeros((27, 2, Z, 3, 4, Z), np.float32)
    for yo in range(2):
        for zo in range(Z):
            for c in range(3):
                for b in range(3):
                    for a in range(3):
                        zi = zo + a - 1
                        if 0 <= zi < Z:
                            taps[(a * 3 + b) * 3 + c, yo, zo, c, yo + b, zi] = 1.0
    return taps.reshape(27, 2 * Z, 12 * Z)


def shifted(value):
    lane = lax.broadcasted_iota(jnp.int32, value.shape, 1)
    width = value.shape[1]
    before = jnp.where(lane == 0, 0.0, pltpu.roll(value, 1, 1))
    after = jnp.where(lane == width - 1, 0.0, pltpu.roll(value, width - 1, 1))
    return before, value, after


def convolutions(image_ref, taps_ref, band_ref, bias_ref, out_ref, band, first, second, third):
    own_index = lax.axis_index("gy")
    last_index = lax.axis_size("gy") - 1
    channels = out_ref.shape[0]
    plane = Z * channels
    lane = lax.broadcasted_iota(jnp.int32, (band_ref.shape[1], plane), 1)
    band[...] = jnp.zeros_like(band)
    for layer in range(2):
        source = band_ref[layer].astype(jnp.float32)
        for zo in range(Z):
            offset = (zo - 1) * channels
            placed = source if offset == 0 else pltpu.roll(source, offset % plane, 1)
            placed = jnp.where((lane >= offset) & (lane < offset + 3 * channels), placed, 0.0)
            placed = placed.astype(jnp.bfloat16)
            for c in range(3):
                for b in range(3):
                    block = placed[(c * 3 + b) * channels : (c * 3 + b + 1) * channels]
                    for yo in range(2):
                        rows = (yo * Z + zo) * channels
                        cols = ((yo + b) * 3 + c) * plane
                        band[layer, rows : rows + channels, cols : cols + plane] = block

    def keep(result, target, pair, pairs, extra_rows):
        result = jnp.maximum(result, 0.0)
        for yo in range(2):
            row = 2 * pair + yo - extra_rows
            part = result[yo * plane : (yo + 1) * plane]
            if row < 0:
                part = jnp.where(own_index > 0, part, 0.0)
            if row >= YB:
                part = jnp.where(own_index < last_index, part, 0.0)
            for c, moved in enumerate(shifted(part)):
                start = ((2 * pair + yo) * 3 + c) * plane
                target[start : start + plane, :] = moved.astype(jnp.bfloat16)

    pieces = shifted(image_ref[...].astype(jnp.float32))
    pairs = YB // 2 + 2
    for pair in range(pairs):
        window = jnp.concatenate(
            [
                piece[2 * pair * Z : (2 * pair + 4) * Z].astype(jnp.bfloat16)
                for piece in pieces
            ],
            axis=0,
        )
        result = jnp.dot(taps_ref[...], window, preferred_element_type=jnp.float32)
        keep(result + bias_ref[:, 0:1], first, pair, pairs, 2)
    depth = 12 * plane
    for pair in range(YB // 2 + 1):
        window = first[6 * pair * plane : 6 * pair * plane + depth, :]
        result = jnp.dot(band[0], window, preferred_element_type=jnp.float32)
        keep(result + bias_ref[:, 1:2], second, pair, YB // 2 + 1, 1)
    for pair in range(YB // 2):
        window = second[6 * pair * plane : 6 * pair * plane + depth, :]
        result = jnp.dot(band[1], window, preferred_element_type=jnp.float32)
        result = jnp.maximum(result + bias_ref[:, 2:3], 0.0)
        for yo in range(2):
            for zo in range(Z):
                rows = (yo * Z + zo) * channels
                start = zo * YB + 2 * pair + yo
                for block in range(third.shape[0]):
                    third[block, pl.ds(start, channels, stride=Z * YB), :] = result[
                        rows : rows + channels, block * 128 : (block + 1) * 128
                    ]
    for block in range(third.shape[0]):
        out_ref[:, :, :, block * 128 : (block + 1) * 128] = (
            third[block].reshape(channels, Z, YB, 128).astype(jnp.bfloat16)
        )


def network(image, w_first, b_first, w_second, b_second, w_third, b_third):
    channels = w_first.shape[0]
    width = image.shape[1]
    plane = Z * channels
    taps = jnp.einsum(
        "ot,trk->rok",
        w_first.reshape(channels, 27),
        first_taps().astype(jnp.bfloat16),
        preferred_element_type=jnp.float32,
    )
    taps = taps.astype(jnp.bfloat16).reshape(2 * plane, 12 * Z)
    weights = jnp.stack([w_second, w_third]).transpose(0, 5, 4, 1, 3, 2)
    weights = jnp.pad(weights, ((0, 0), (0, 0), (0, 0), (0, 0), (0, 1), (0, 0)))
    weights = weights.reshape(2, 9 * channels, 4 * channels)
    biases = jnp.tile(jnp.stack([b_first, b_second, b_third], axis=1), (2 * Z, 1))
    vmem = pl.BlockSpec(memory_space=pltpu.VMEM)
    return pl.pallas_call(
        convolutions,
        out_shape=jax.ShapeDtypeStruct((channels, Z, YB, width), jnp.bfloat16),
        in_specs=[vmem] * 4,
        out_specs=vmem,
        scratch_shapes=[
            pltpu.VMEM((2, 2 * plane, 12 * plane), jnp.bfloat16),
            pltpu.VMEM((3 * plane * (YB + 4), width), jnp.bfloat16),
            pltpu.VMEM((3 * plane * (YB + 2), width), jnp.bfloat16),
            pltpu.VMEM((width // 128, plane * YB, 128), jnp.float32),
        ],
        compiler_params=pltpu.CompilerParams(vmem_limit_bytes=48 << 20),
        name="network",
    )(image, taps, weights, biases)


def on_device(
    tiles,
    entry_dest,
    entry_tile,
    entry_z,
    entry_xb,
    entry_ky,
    entry_kx,
    wy_table,
    wx_table,
    w_first,
    b_first,
    w_second,
    b_second,
    w_third,
    b_third,
):
    rows = rendered_window(
        tiles,
        (entry_dest, entry_tile, entry_z, entry_xb, entry_ky, entry_kx),
        wy_table,
        wx_table,
    )
    return network(rows, w_first, b_first, w_second, b_second, w_third, b_third)


def solution(mesh):
    return jax.shard_map(
        on_device,
        mesh=mesh,
        in_specs=(
            P(("groups", "gy"), None, None),
            P("groups", None),
            P("groups"),
            P("groups"),
            P("groups"),
            P("groups"),
            P("groups"),
            P(),
            P(),
            P(),
            P(),
            P(),
            P(),
            P(),
            P(),
        ),
        out_specs=P(None, "groups", "gy", None),
        check_vma=False,
    )
```

```python
import jax
import jax.numpy as jnp
import numpy as np
from jax import lax
from jax.experimental import pallas as pl
from jax.experimental.pallas import tpu as pltpu
from jax.sharding import PartitionSpec as P

X = 512
YB = 8
Z = 4
CAP = 4
HALO = 3


MESH = pl.DeviceIdType.MESH
GROUP = 4
NT = (((1,), (1,)), ((), ()))


def message_row(line):
    own, before = line < CAP * YB, line < CAP * (YB + HALO)
    side = jnp.where(before, line - CAP * YB, line - CAP * (YB + HALO))
    offset = jnp.where(own, 0, jnp.where(before, -1, 1))
    slot = jnp.where(own, line // YB, side // HALO)
    rest = jnp.where(own, line % YB, side % HALO)
    row = jnp.where(own | ~before, rest, rest + YB - HALO)
    used = line < CAP * (YB + 2 * HALO)
    return jnp.where(used, offset * CAP + slot, -1000), row, row + offset * YB + HALO


def iota(shape, axis):
    return lax.broadcasted_iota(jnp.int32, shape, axis)


def onehot(mask):
    return jnp.where(mask, 1.0, 0.0).astype(jnp.bfloat16)


def arrange(spots_ref, w_first_ref, deep, b_first_ref, b_second_ref, b_third_ref, taps_ref, band, bias_ref):
    channels = b_first_ref.shape[1]
    plane = Z * channels
    first = jnp.concatenate(
        [w_first_ref[k].astype(jnp.float32) for k in range(w_first_ref.shape[0])], axis=0
    )
    first = lax.dot_general(
        first.astype(jnp.bfloat16),
        spots_ref[...],
        (((0,), (0,)), ((), ())),
        preferred_element_type=jnp.float32,
    ).astype(jnp.bfloat16)
    for block in range(2 * Z):
        taps_ref[block * channels : (block + 1) * channels, :] = first[
            :, block * 128 : (block + 1) * 128
        ]
    lane = iota((2 * plane, 128), 1)
    biases = jnp.zeros((2 * plane, 128), jnp.float32)
    square = (channels, channels)
    for layer, b_ref in enumerate((b_first_ref, b_second_ref, b_third_ref)):
        diagonal = jnp.where(iota(square, 0) == iota(square, 1), b_ref[...], 0.0)
        column = jnp.sum(diagonal, axis=1, keepdims=True)
        biases = jnp.where(lane == layer, jnp.concatenate([column] * (2 * Z), axis=0), biases)
    bias_ref[...] = biases
    lane = iota((9 * channels, plane), 1)
    empty = jnp.zeros((channels, plane), jnp.bfloat16)
    for layer in range(2):
        source = jnp.concatenate(
            [
                jnp.concatenate(
                    [deep[layer, (a * 3 + b) * 3 + c].astype(jnp.float32) for a in range(3)]
                    + [jnp.zeros(square, jnp.float32)],
                    axis=1,
                )
                for c in range(3)
                for b in range(3)
            ],
            axis=0,
        )
        for zo in range(Z):
            offset = (zo - 1) * channels
            placed = source if offset == 0 else pltpu.roll(source, offset % plane, 1)
            placed = jnp.where((lane >= offset) & (lane < offset + 3 * channels), placed, 0.0)
            placed = placed.astype(jnp.bfloat16)
            for c in range(3):
                for yo in range(2):
                    rows = (yo * Z + zo) * channels
                    for yi in range(4):
                        b = yi - yo
                        cols = (yi * 3 + c) * plane
                        block = empty
                        if 0 <= b < 3:
                            block = placed[(c * 3 + b) * channels : (c * 3 + b + 1) * channels]
                        band[layer, rows : rows + channels, cols : cols + plane] = block


def render(
    tiles_ref, dest_ref, tile_ref, z_ref, xb_ref, ky_ref, kx_ref, wy_ref, wx_hbm,
    spots_ref, w_first_ref, w_second_hbm, w_third_hbm, b_first_ref, b_second_ref, b_third_ref,
    image_ref, taps_ref, band, bias_ref,
    fields, sent, arrived, wx_ref, deep, send_sem, recv_sem, load_sem,
):
    count = lax.axis_size("gy")
    own_index = lax.axis_index("gy")
    lines = sent.shape[1]
    live = CAP * (YB + 2 * HALO)
    lanes = dest_ref.shape[1]
    per_device = dest_ref.shape[0] * lanes // count
    window = YB + 2 * HALO
    order = sorted(range(1, count), key=lambda i: -min(i, count - i))

    loads = [
        pltpu.make_async_copy(w_second_hbm, deep.at[0], load_sem.at[0]),
        pltpu.make_async_copy(w_third_hbm, deep.at[1], load_sem.at[1]),
        pltpu.make_async_copy(wx_hbm, wx_ref, load_sem.at[2]),
    ]
    for load in loads:
        load.start()
    arrived[:, live - live % 16 :, :] = jnp.zeros(
        (count, lines - live + live % 16, arrived.shape[2]), jnp.bfloat16
    )
    barrier = pltpu.get_barrier_semaphore()
    for i in order:
        pl.semaphore_signal(
            barrier, inc=1, device_id={"gy": lax.rem(own_index + i, count)}, device_id_type=MESH
        )

    dest = dest_ref[...]
    place = iota(dest.shape, 1) % per_device
    rank = jnp.zeros_like(dest)
    for step in range(1, per_device):
        same = (pltpu.roll(dest, step, 1) == dest) & (place >= step)
        rank = rank + jnp.where(same, 1, 0)
    rows = [
        dest * CAP + rank,
        ky_ref[...],
        tile_ref[...],
        kx_ref[...] + 1,
        xb_ref[...] * (window * Z) + z_ref[...] + 1,
    ]
    rows = [row.astype(jnp.float32) for row in rows]
    rows = rows + [jnp.zeros_like(rows[0])] * 3
    span = GROUP * per_device // lanes
    for group in range(count // GROUP):
        for part in range(span):
            line = group * span + part
            fields[group, :, part * lanes : (part + 1) * lanes] = jnp.concatenate(
                [row[line : line + 1] for row in rows], axis=0
            )

    own_group = own_index // GROUP
    mine = fields[own_group].astype(jnp.bfloat16)
    samples = per_device * YB
    expand = onehot(
        iota((samples, GROUP * per_device), 1)
        == iota((samples, GROUP * per_device), 0) // YB + (own_index % GROUP) * per_device
    )
    column = lax.dot_general(expand, mine, NT, preferred_element_type=jnp.float32)
    along = lax.dot_general(mine, expand, NT, preferred_element_type=jnp.float32)
    blocks, tile_rows = wy_ref.shape
    spot = iota((samples, blocks), 1)
    picked = onehot(
        ((spot // YB).astype(jnp.float32) == column[:, 1:2])
        & (spot % YB == iota((samples, blocks), 0) % YB)
    )
    vertical = jnp.dot(picked, wy_ref[...], preferred_element_type=jnp.float32)
    pixels = tiles_ref.shape[0]
    repeat = onehot(iota((tile_rows, pixels), 1) % tile_rows == iota((tile_rows, pixels), 0))
    vertical = jnp.dot(
        vertical.astype(jnp.bfloat16), repeat, preferred_element_type=jnp.float32
    )
    chosen = (iota((samples, pixels), 1) // tile_rows).astype(jnp.float32) == column[:, 2:3]
    vertical = jnp.where(chosen, vertical, 0.0).astype(jnp.bfloat16)
    row_samples = jnp.dot(
        vertical, tiles_ref[...], preferred_element_type=jnp.float32
    ).astype(jnp.bfloat16)

    key, row, _ = message_row(iota((lines, samples), 0))
    wanted = along[0:1, :] - key.astype(jnp.float32)
    wanted = jnp.where(row == iota((lines, samples), 1) % YB, wanted, -4000.0)

    def message(number):
        target = lax.rem(own_index + number, count)
        return onehot(wanted == (target * CAP).astype(jnp.float32))

    copies = []
    order = order + [0]
    for start in range(0, count, GROUP):
        numbers = order[start : start + GROUP]
        packed = jnp.dot(
            jnp.concatenate([message(number) for number in numbers], axis=0),
            row_samples,
            preferred_element_type=jnp.float32,
        ).astype(jnp.bfloat16)
        for part, number in enumerate(numbers):
            block = packed[part * lines : (part + 1) * lines]
            if number == 0:
                arrived[own_index] = block
            else:
                sent[number] = block
        if start == 0:
            pl.semaphore_wait(barrier, count - 1)
        for number in numbers:
            if number > 0:
                copy = pltpu.make_async_remote_copy(
                    src_ref=sent.at[number, 0:live],
                    dst_ref=arrived.at[own_index, 0:live],
                    send_sem=send_sem.at[number],
                    recv_sem=recv_sem.at[number],
                    device_id={"gy": lax.rem(own_index + number, count)},
                    device_id_type=MESH,
                )
                copy.start()
                copies.append(copy)

    depth = GROUP * lines
    entries = GROUP * per_device
    total = None
    horizontals = wx_ref.shape[0] // wx_ref.shape[1]
    key, _, window_row = message_row(iota((depth, entries), 0) % lines)
    sources = iota((depth, entries), 0) // lines == iota((depth, entries), 1) // per_device
    wanted_key = jnp.where(sources, key + own_index * CAP, -5000).astype(jnp.float32)
    _, _, target_row = message_row(iota((1, depth), 1) % lines)
    x_blocks = image_ref.shape[1] // wx_ref.shape[1]
    targets = x_blocks * window * Z
    meta = []
    for group in range(count // GROUP):
        held = fields[group]
        match = onehot(held[0:1, :] == wanted_key)
        held = held.astype(jnp.bfloat16)
        source = lax.dot_general(match, held, NT, preferred_element_type=jnp.float32)
        target = lax.dot_general(held, match, NT, preferred_element_type=jnp.float32)
        code = target[4:5, :]
        code = jnp.where(
            code > 0.5, code - 1.0 + (target_row * Z).astype(jnp.float32), -1.0
        )
        placed = onehot(iota((targets, depth), 0).astype(jnp.float32) == code)
        meta.append((source[:, 3:4], placed))
    for load in loads:
        load.wait()
    arrange(spots_ref, w_first_ref, deep, b_first_ref, b_second_ref, b_third_ref, taps_ref, band, bias_ref)
    for copy in copies:
        copy.wait()
    for group in range(count // GROUP):
        horizontal, placed = meta[group]
        samples_in = jnp.concatenate(
            [arrived[group * GROUP + part] for part in range(GROUP)], axis=0
        ).astype(jnp.float32)
        spread = jnp.concatenate(
            [
                jnp.where(horizontal == float(block + 1), samples_in, 0.0).astype(jnp.bfloat16)
                for block in range(horizontals)
            ],
            axis=1,
        )
        patches = jnp.dot(spread, wx_ref[...], preferred_element_type=jnp.float32)
        high = patches.astype(jnp.bfloat16)
        rest = patches - high.astype(jnp.float32)
        middle = rest.astype(jnp.bfloat16)
        low = (rest - middle.astype(jnp.float32)).astype(jnp.bfloat16)
        part = jnp.dot(
            placed, jnp.concatenate([high, middle, low], axis=1), preferred_element_type=jnp.float32
        )
        total = part if total is None else total + part
    columns = wx_ref.shape[1]
    total = total[:, :columns] + total[:, columns : 2 * columns] + total[:, 2 * columns :]
    for block in range(x_blocks):
        image_ref[:, block * columns : (block + 1) * columns] = total[
            block * window * Z : (block + 1) * window * Z
        ].astype(jnp.bfloat16)


def rendered_window(tiles, entries, wy_table, wx_table, weights, biases):
    count = lax.axis_size("gy")
    tiles_dev, tile_rows, tile_cols = tiles.shape
    lines = -(-CAP * (YB + 2 * HALO) // 16) * 16
    per_device = entries[0].size // count
    entries = [entry.reshape(-1, 128) for entry in entries]
    vmem = pl.BlockSpec(memory_space=pltpu.VMEM)
    hbm = pl.BlockSpec(memory_space=pl.ANY)
    channels = biases[0].shape[0]
    plane = Z * channels
    return pl.pallas_call(
        render,
        out_shape=[
            jax.ShapeDtypeStruct(((YB + 2 * HALO) * Z, X), jnp.bfloat16),
            jax.ShapeDtypeStruct((2 * plane, 128), jnp.bfloat16),
            jax.ShapeDtypeStruct((2, 2 * plane, 12 * plane), jnp.bfloat16),
            jax.ShapeDtypeStruct((2 * plane, 128), jnp.float32),
        ],
        in_specs=[vmem] * 8 + [hbm] + [vmem] * 2 + [hbm] * 2 + [vmem] * 3,
        out_specs=[vmem] * 4,
        scratch_shapes=[
            pltpu.VMEM((count // GROUP, 8, GROUP * per_device), jnp.float32),
            pltpu.VMEM((count, lines, tile_cols), jnp.bfloat16),
            pltpu.VMEM((count, lines, tile_cols), jnp.bfloat16),
            pltpu.VMEM((wx_table.shape[0] * wx_table.shape[1], tile_cols), jnp.bfloat16),
            pltpu.VMEM((2, 27, channels, channels), jnp.bfloat16),
            pltpu.SemaphoreType.DMA((count,)),
            pltpu.SemaphoreType.DMA((count,)),
            pltpu.SemaphoreType.DMA((3,)),
        ],
        compiler_params=pltpu.CompilerParams(
            collective_id=0, has_side_effects=True, vmem_limit_bytes=48 << 20
        ),
        name="render",
    )(
        tiles.reshape(tiles_dev * tile_rows, tile_cols),
        *entries,
        wy_table.reshape(-1, tile_rows),
        wx_table.reshape(-1, tile_cols),
        first_taps().astype(jnp.bfloat16),
        weights[0].transpose(1, 2, 3, 4, 0).reshape(9, 3, channels),
        *[weight.transpose(2, 3, 4, 0, 1).reshape(27, channels, channels) for weight in weights[1:]],
        *[bias.reshape(1, channels) for bias in biases],
    )


def first_taps():
    taps = np.zeros((27, 2, Z, 3, 4, Z), np.float32)
    for yo in range(2):
        for zo in range(Z):
            for c in range(3):
                for b in range(3):
                    for a in range(3):
                        zi = zo + a - 1
                        if 0 <= zi < Z:
                            taps[(a * 3 + b) * 3 + c, yo, zo, c, yo + b, zi] = 1.0
    taps = taps.reshape(27, 2 * Z, 12 * Z)
    return np.pad(taps, ((0, 0), (0, 0), (0, 128 - 12 * Z))).reshape(27, -1)


def shifted(value):
    lane = lax.broadcasted_iota(jnp.int32, value.shape, 1)
    width = value.shape[1]
    before = jnp.where(lane == 0, 0.0, pltpu.roll(value, 1, 1))
    after = jnp.where(lane == width - 1, 0.0, pltpu.roll(value, width - 1, 1))
    return before, value, after


def convolutions(image_ref, taps_ref, band, bias_ref, out_ref, first, second, third):
    own_index = lax.axis_index("gy")
    last_index = lax.axis_size("gy") - 1
    channels = out_ref.shape[0]
    plane = Z * channels
    def keep(result, target, pair, pairs, extra_rows):
        result = jnp.maximum(result, 0.0)
        for yo in range(2):
            row = 2 * pair + yo - extra_rows
            part = result[yo * plane : (yo + 1) * plane]
            if row < 0:
                part = jnp.where(own_index > 0, part, 0.0)
            if row >= YB:
                part = jnp.where(own_index < last_index, part, 0.0)
            for c, moved in enumerate(shifted(part)):
                start = ((2 * pair + yo) * 3 + c) * plane
                target[start : start + plane, :] = moved.astype(jnp.bfloat16)

    pieces = shifted(image_ref[...].astype(jnp.float32))
    pairs = YB // 2 + 2
    for pair in range(pairs):
        window = jnp.concatenate(
            [
                piece[2 * pair * Z : (2 * pair + 4) * Z].astype(jnp.bfloat16)
                for piece in pieces
            ],
            axis=0,
        )
        result = jnp.dot(taps_ref[:, : 12 * Z], window, preferred_element_type=jnp.float32)
        keep(result + bias_ref[:, 0:1], first, pair, pairs, 2)
    depth = 12 * plane
    for pair in range(YB // 2 + 1):
        window = first[6 * pair * plane : 6 * pair * plane + depth, :]
        result = jnp.dot(band[0], window, preferred_element_type=jnp.float32)
        keep(result + bias_ref[:, 1:2], second, pair, YB // 2 + 1, 1)
    half = min(256, third.shape[0] * 128)
    for start_x in range(0, third.shape[0] * 128, half):
        blocks = range(start_x // 128, (start_x + half) // 128)
        for pair in range(YB // 2):
            rows = 6 * pair * plane
            window = second[rows : rows + depth, start_x : start_x + half]
            result = jnp.dot(band[1], window, preferred_element_type=jnp.float32)
            result = jnp.maximum(result + bias_ref[:, 2:3], 0.0)
            for yo in range(2):
                for zo in range(Z):
                    rows = (yo * Z + zo) * channels
                    start = zo * YB + 2 * pair + yo
                    for part, block in enumerate(blocks):
                        third[block, pl.ds(start, channels, stride=Z * YB), :] = result[
                            rows : rows + channels, part * 128 : (part + 1) * 128
                        ]
        for block in blocks:
            out_ref[:, :, :, block * 128 : (block + 1) * 128] = (
                third[block].reshape(channels, Z, YB, 128).astype(jnp.bfloat16)
            )


def network(image, taps, band, biases, channels):
    width = image.shape[1]
    plane = Z * channels
    vmem = pl.BlockSpec(memory_space=pltpu.VMEM)
    return pl.pallas_call(
        convolutions,
        out_shape=jax.ShapeDtypeStruct((channels, Z, YB, width), jnp.bfloat16),
        in_specs=[vmem] * 4,
        out_specs=vmem,
        scratch_shapes=[
            pltpu.VMEM((3 * plane * (YB + 4), width), jnp.bfloat16),
            pltpu.VMEM((3 * plane * (YB + 2), width), jnp.bfloat16),
            pltpu.VMEM((width // 128, plane * YB, 128), jnp.float32),
        ],
        compiler_params=pltpu.CompilerParams(vmem_limit_bytes=48 << 20),
        name="network",
    )(image, taps, band, biases)


def on_device(
    tiles,
    entry_dest,
    entry_tile,
    entry_z,
    entry_xb,
    entry_ky,
    entry_kx,
    wy_table,
    wx_table,
    w_first,
    b_first,
    w_second,
    b_second,
    w_third,
    b_third,
):
    prepared = rendered_window(
        tiles,
        (entry_dest, entry_tile, entry_z, entry_xb, entry_ky, entry_kx),
        wy_table,
        wx_table,
        (w_first, w_second, w_third),
        (b_first, b_second, b_third),
    )
    return network(*prepared, w_first.shape[0])


def solution(mesh):
    return jax.shard_map(
        on_device,
        mesh=mesh,
        in_specs=(
            P(("groups", "gy"), None, None),
            P("groups", None),
            P("groups"),
            P("groups"),
            P("groups"),
            P("groups"),
            P("groups"),
            P(),
            P(),
            P(),
            P(),
            P(),
            P(),
            P(),
            P(),
        ),
        out_specs=P(None, "groups", "gy", None),
        check_vma=False,
    )
```

```python
import jax
import jax.numpy as jnp
import numpy as np
from jax import lax
from jax.experimental import pallas as pl
from jax.experimental.pallas import tpu as pltpu
from jax.sharding import PartitionSpec as P

X = 512
YB = 8
Z = 4
CAP = 4
HALO = 3
VMEM_BYTES = 67043328


MESH = pl.DeviceIdType.MESH
GROUP = 4
NT = (((1,), (1,)), ((), ()))


def message_row(line):
    own, before = line < CAP * YB, line < CAP * (YB + HALO)
    side = jnp.where(before, line - CAP * YB, line - CAP * (YB + HALO))
    offset = jnp.where(own, 0, jnp.where(before, -1, 1))
    slot = jnp.where(own, line // YB, side // HALO)
    rest = jnp.where(own, line % YB, side % HALO)
    row = jnp.where(own | ~before, rest, rest + YB - HALO)
    used = line < CAP * (YB + 2 * HALO)
    return jnp.where(used, offset * CAP + slot, -1000), row, row + offset * YB + HALO


def iota(shape, axis):
    return lax.broadcasted_iota(jnp.int32, shape, axis)


def onehot(mask):
    return jnp.where(mask, 1.0, 0.0).astype(jnp.bfloat16)


def arrange(spots_ref, w_first_ref, deep, b_first_ref, b_second_ref, b_third_ref, taps_ref, band, bias_ref):
    channels = b_first_ref.shape[1]
    plane = Z * channels
    first = jnp.concatenate(
        [w_first_ref[k].astype(jnp.float32) for k in range(w_first_ref.shape[0])], axis=0
    )
    first = lax.dot_general(
        first.astype(jnp.bfloat16),
        spots_ref[...],
        (((0,), (0,)), ((), ())),
        preferred_element_type=jnp.float32,
    ).astype(jnp.bfloat16)
    for block in range(2 * Z):
        taps_ref[block * channels : (block + 1) * channels, :] = first[
            :, block * 128 : (block + 1) * 128
        ]
    lane = iota((2 * plane, 128), 1)
    biases = jnp.zeros((2 * plane, 128), jnp.float32)
    square = (channels, channels)
    for layer, b_ref in enumerate((b_first_ref, b_second_ref, b_third_ref)):
        diagonal = jnp.where(iota(square, 0) == iota(square, 1), b_ref[...], 0.0)
        column = jnp.sum(diagonal, axis=1, keepdims=True)
        biases = jnp.where(lane == layer, jnp.concatenate([column] * (2 * Z), axis=0), biases)
    bias_ref[...] = biases
    lane = iota((9 * channels, plane), 1)
    empty = jnp.zeros((channels, plane), jnp.bfloat16)
    for layer in range(2):
        source = jnp.concatenate(
            [
                jnp.concatenate(
                    [deep[layer][(a * 3 + b) * 3 + c].astype(jnp.float32) for a in range(3)]
                    + [jnp.zeros(square, jnp.float32)],
                    axis=1,
                )
                for c in range(3)
                for b in range(3)
            ],
            axis=0,
        )
        for zo in range(Z):
            offset = (zo - 1) * channels
            placed = source if offset == 0 else pltpu.roll(source, offset % plane, 1)
            placed = jnp.where((lane >= offset) & (lane < offset + 3 * channels), placed, 0.0)
            placed = placed.astype(jnp.bfloat16)
            for c in range(3):
                for yo in range(2):
                    rows = (yo * Z + zo) * channels
                    for yi in range(4):
                        b = yi - yo
                        cols = (yi * 3 + c) * plane
                        block = empty
                        if 0 <= b < 3:
                            block = placed[(c * 3 + b) * channels : (c * 3 + b + 1) * channels]
                        band[layer, rows : rows + channels, cols : cols + plane] = block


def render(*refs):
    inputs = refs[:16]
    image_ref = refs[16]
    stored = refs[17:20]
    held_inputs = refs[20:36]
    taps_ref, band, bias_ref, fields, sent, arrived, send_sem, recv_sem, load_sem = refs[36:]
    loads = [
        pltpu.make_async_copy(source, target, load_sem.at[number])
        for number, (source, target) in enumerate(zip(inputs, held_inputs))
    ]
    for load in loads:
        load.start()
    dest_ref, tile_ref, z_ref, xb_ref, ky_ref, kx_ref, wy_ref, tiles_ref = held_inputs[:8]
    wx_ref, spots_ref, w_first_ref, w_second_ref, w_third_ref = held_inputs[8:13]
    b_first_ref, b_second_ref, b_third_ref = held_inputs[13:]
    count = lax.axis_size("gy")
    own_index = lax.axis_index("gy")
    lines = sent.shape[1]
    live = CAP * (YB + 2 * HALO)
    lanes = dest_ref.shape[1]
    per_device = dest_ref.shape[0] * lanes // count
    window = YB + 2 * HALO
    order = sorted(range(1, count), key=lambda i: -min(i, count - i))

    arrived[:, live - live % 16 :, :] = jnp.zeros(
        (count, lines - live + live % 16, arrived.shape[2]), jnp.bfloat16
    )
    barrier = pltpu.get_barrier_semaphore()
    for i in order:
        pl.semaphore_signal(
            barrier, inc=1, device_id={"gy": lax.rem(own_index + i, count)}, device_id_type=MESH
        )

    for load in loads[:6]:
        load.wait()
    dest = dest_ref[...]
    place = iota(dest.shape, 1) % per_device
    rank = jnp.zeros_like(dest)
    for step in range(1, per_device):
        same = (pltpu.roll(dest, step, 1) == dest) & (place >= step)
        rank = rank + jnp.where(same, 1, 0)
    rows = [
        dest * CAP + rank,
        ky_ref[...],
        tile_ref[...],
        kx_ref[...] + 1,
        xb_ref[...] * (window * Z) + z_ref[...] + 1,
    ]
    rows = [row.astype(jnp.float32) for row in rows]
    rows = rows + [jnp.zeros_like(rows[0])] * 3
    span = GROUP * per_device // lanes
    for group in range(count // GROUP):
        for part in range(span):
            line = group * span + part
            fields[group, :, part * lanes : (part + 1) * lanes] = jnp.concatenate(
                [row[line : line + 1] for row in rows], axis=0
            )

    for load in loads[6:8]:
        load.wait()
    own_group = own_index // GROUP
    mine = fields[own_group].astype(jnp.bfloat16)
    samples = per_device * YB
    expand = onehot(
        iota((samples, GROUP * per_device), 1)
        == iota((samples, GROUP * per_device), 0) // YB + (own_index % GROUP) * per_device
    )
    column = lax.dot_general(expand, mine, NT, preferred_element_type=jnp.float32)
    along = lax.dot_general(mine, expand, NT, preferred_element_type=jnp.float32)
    blocks, tile_rows = wy_ref.shape
    spot = iota((samples, blocks), 1)
    picked = onehot(
        ((spot // YB).astype(jnp.float32) == column[:, 1:2])
        & (spot % YB == iota((samples, blocks), 0) % YB)
    )
    vertical = jnp.dot(picked, wy_ref[...], preferred_element_type=jnp.float32)
    pixels = tiles_ref.shape[0]
    repeat = onehot(iota((tile_rows, pixels), 1) % tile_rows == iota((tile_rows, pixels), 0))
    vertical = jnp.dot(
        vertical.astype(jnp.bfloat16), repeat, preferred_element_type=jnp.float32
    )
    chosen = (iota((samples, pixels), 1) // tile_rows).astype(jnp.float32) == column[:, 2:3]
    vertical = jnp.where(chosen, vertical, 0.0).astype(jnp.bfloat16)
    row_samples = jnp.dot(
        vertical, tiles_ref[...], preferred_element_type=jnp.float32
    ).astype(jnp.bfloat16)

    key, row, _ = message_row(iota((lines, samples), 0))
    wanted = along[0:1, :] - key.astype(jnp.float32)
    wanted = jnp.where(row == iota((lines, samples), 1) % YB, wanted, -4000.0)

    def message(number):
        target = lax.rem(own_index + number, count)
        return onehot(wanted == (target * CAP).astype(jnp.float32))

    copies = []
    order = order + [0]
    for start in range(0, count, GROUP):
        numbers = order[start : start + GROUP]
        packed = jnp.dot(
            jnp.concatenate([message(number) for number in numbers], axis=0),
            row_samples,
            preferred_element_type=jnp.float32,
        ).astype(jnp.bfloat16)
        for part, number in enumerate(numbers):
            block = packed[part * lines : (part + 1) * lines]
            if number == 0:
                arrived[own_index] = block
            else:
                sent[number] = block
        if start == 0:
            pl.semaphore_wait(barrier, count - 1)
        for number in numbers:
            if number > 0:
                copy = pltpu.make_async_remote_copy(
                    src_ref=sent.at[number, 0:live],
                    dst_ref=arrived.at[own_index, 0:live],
                    send_sem=send_sem.at[number],
                    recv_sem=recv_sem.at[number],
                    device_id={"gy": lax.rem(own_index + number, count)},
                    device_id_type=MESH,
                )
                copy.start()
                copies.append(copy)

    depth = GROUP * lines
    entries = GROUP * per_device
    total = None
    horizontals = wx_ref.shape[0] // wx_ref.shape[1]
    key, _, window_row = message_row(iota((depth, entries), 0) % lines)
    sources = iota((depth, entries), 0) // lines == iota((depth, entries), 1) // per_device
    wanted_key = jnp.where(sources, key + own_index * CAP, -5000).astype(jnp.float32)
    _, _, target_row = message_row(iota((1, depth), 1) % lines)
    x_blocks = image_ref.shape[1] // wx_ref.shape[1]
    targets = x_blocks * window * Z
    meta = []
    for group in range(count // GROUP):
        held = fields[group]
        match = onehot(held[0:1, :] == wanted_key)
        held = held.astype(jnp.bfloat16)
        source = lax.dot_general(match, held, NT, preferred_element_type=jnp.float32)
        target = lax.dot_general(held, match, NT, preferred_element_type=jnp.float32)
        code = target[4:5, :]
        code = jnp.where(
            code > 0.5, code - 1.0 + (target_row * Z).astype(jnp.float32), -1.0
        )
        placed = onehot(iota((targets, depth), 0).astype(jnp.float32) == code)
        meta.append((source[:, 3:4], placed))
    for load in loads[8:]:
        load.wait()
    deep = (w_second_ref, w_third_ref)
    arrange(spots_ref, w_first_ref, deep, b_first_ref, b_second_ref, b_third_ref, taps_ref, band, bias_ref)
    stores = [
        pltpu.make_async_copy(source, target, load_sem.at[len(inputs) + number])
        for number, (source, target) in enumerate(zip((taps_ref, band, bias_ref), stored))
    ]
    for store in stores:
        store.start()
    for copy in copies:
        copy.wait()
    for group in range(count // GROUP):
        horizontal, placed = meta[group]
        samples_in = jnp.concatenate(
            [arrived[group * GROUP + part] for part in range(GROUP)], axis=0
        ).astype(jnp.float32)
        spread = jnp.concatenate(
            [
                jnp.where(horizontal == float(block + 1), samples_in, 0.0).astype(jnp.bfloat16)
                for block in range(horizontals)
            ],
            axis=1,
        )
        patches = jnp.dot(spread, wx_ref[...], preferred_element_type=jnp.float32)
        high = patches.astype(jnp.bfloat16)
        rest = patches - high.astype(jnp.float32)
        middle = rest.astype(jnp.bfloat16)
        low = (rest - middle.astype(jnp.float32)).astype(jnp.bfloat16)
        part = jnp.dot(
            placed, jnp.concatenate([high, middle, low], axis=1), preferred_element_type=jnp.float32
        )
        total = part if total is None else total + part
    columns = wx_ref.shape[1]
    total = total[:, :columns] + total[:, columns : 2 * columns] + total[:, 2 * columns :]
    for block in range(x_blocks):
        image_ref[:, block * columns : (block + 1) * columns] = total[
            block * window * Z : (block + 1) * window * Z
        ].astype(jnp.bfloat16)
    for store in stores:
        store.wait()


def rendered_window(tiles, entries, wy_table, wx_table, weights, biases):
    count = lax.axis_size("gy")
    tiles_dev, tile_rows, tile_cols = tiles.shape
    lines = -(-CAP * (YB + 2 * HALO) // 16) * 16
    per_device = entries[0].size // count
    entries = [entry.reshape(-1, 128) for entry in entries]
    vmem = pl.BlockSpec(memory_space=pltpu.VMEM)
    hbm = pl.BlockSpec(memory_space=pltpu.HBM)
    channels = biases[0].shape[0]
    plane = Z * channels
    inputs = [
        *entries,
        wy_table.reshape(-1, tile_rows),
        tiles.reshape(tiles_dev * tile_rows, tile_cols),
        wx_table.reshape(-1, tile_cols),
        jnp.asarray(first_taps(), jnp.bfloat16),
        weights[0].transpose(1, 2, 3, 4, 0).reshape(9, 3, channels),
        *[weight.transpose(2, 3, 4, 0, 1).reshape(27, channels, channels) for weight in weights[1:]],
        *[bias.reshape(1, channels) for bias in biases],
    ]
    return pl.pallas_call(
        render,
        out_shape=[
            jax.ShapeDtypeStruct(((YB + 2 * HALO) * Z, X), jnp.bfloat16),
            jax.ShapeDtypeStruct((2 * plane, 128), jnp.bfloat16),
            jax.ShapeDtypeStruct((2, 2 * plane, 12 * plane), jnp.bfloat16),
            jax.ShapeDtypeStruct((2 * plane, 128), jnp.float32),
        ],
        in_specs=[hbm] * len(inputs),
        out_specs=[vmem] + [hbm] * 3,
        scratch_shapes=[pltpu.VMEM(value.shape, value.dtype) for value in inputs]
        + [
            pltpu.VMEM((2 * plane, 128), jnp.bfloat16),
            pltpu.VMEM((2, 2 * plane, 12 * plane), jnp.bfloat16),
            pltpu.VMEM((2 * plane, 128), jnp.float32),
            pltpu.VMEM((count // GROUP, 8, GROUP * per_device), jnp.float32),
            pltpu.VMEM((count, lines, tile_cols), jnp.bfloat16),
            pltpu.VMEM((count, lines, tile_cols), jnp.bfloat16),
            pltpu.SemaphoreType.DMA((count,)),
            pltpu.SemaphoreType.DMA((count,)),
            pltpu.SemaphoreType.DMA((len(inputs) + 3,)),
        ],
        compiler_params=pltpu.CompilerParams(
            collective_id=0, has_side_effects=True, vmem_limit_bytes=VMEM_BYTES
        ),
        name="render",
    )(*inputs)


def first_taps():
    taps = np.zeros((27, 2, Z, 3, 4, Z), np.float32)
    for yo in range(2):
        for zo in range(Z):
            for c in range(3):
                for b in range(3):
                    for a in range(3):
                        zi = zo + a - 1
                        if 0 <= zi < Z:
                            taps[(a * 3 + b) * 3 + c, yo, zo, c, yo + b, zi] = 1.0
    taps = taps.reshape(27, 2 * Z, 12 * Z)
    return np.pad(taps, ((0, 0), (0, 0), (0, 128 - 12 * Z))).reshape(27, -1)


def shifted(value):
    lane = lax.broadcasted_iota(jnp.int32, value.shape, 1)
    width = value.shape[1]
    before = jnp.where(lane == 0, 0.0, pltpu.roll(value, 1, 1))
    after = jnp.where(lane == width - 1, 0.0, pltpu.roll(value, width - 1, 1))
    return before, value, after


def convolutions(
    image_hbm, taps_hbm, band_hbm, bias_hbm, out_ref,
    image_ref, taps_ref, band, bias_ref, first, second, third, load_sem,
):
    loads = [
        pltpu.make_async_copy(source, target, load_sem.at[number])
        for number, (source, target) in enumerate(
            (
                (image_hbm, image_ref),
                (taps_hbm, taps_ref),
                (bias_hbm, bias_ref),
                (band_hbm, band),
            )
        )
    ]
    for load in loads:
        load.start()
    for load in loads[:3]:
        load.wait()
    own_index = lax.axis_index("gy")
    last_index = lax.axis_size("gy") - 1
    channels = out_ref.shape[0]
    plane = Z * channels
    def keep(result, target, pair, pairs, extra_rows):
        result = jnp.maximum(result, 0.0)
        for yo in range(2):
            row = 2 * pair + yo - extra_rows
            part = result[yo * plane : (yo + 1) * plane]
            if row < 0:
                part = jnp.where(own_index > 0, part, 0.0)
            if row >= YB:
                part = jnp.where(own_index < last_index, part, 0.0)
            for c, moved in enumerate(shifted(part)):
                start = ((2 * pair + yo) * 3 + c) * plane
                target[start : start + plane, :] = moved.astype(jnp.bfloat16)

    pieces = shifted(image_ref[...].astype(jnp.float32))
    pairs = YB // 2 + 2
    for pair in range(pairs):
        window = jnp.concatenate(
            [
                piece[2 * pair * Z : (2 * pair + 4) * Z].astype(jnp.bfloat16)
                for piece in pieces
            ],
            axis=0,
        )
        result = jnp.dot(taps_ref[:, : 12 * Z], window, preferred_element_type=jnp.float32)
        keep(result + bias_ref[:, 0:1], first, pair, pairs, 2)
    depth = 12 * plane
    loads[3].wait()
    for pair in range(YB // 2 + 1):
        window = first[6 * pair * plane : 6 * pair * plane + depth, :]
        result = jnp.dot(band[0], window, preferred_element_type=jnp.float32)
        keep(result + bias_ref[:, 1:2], second, pair, YB // 2 + 1, 1)
    for pair in range(YB // 2):
        window = second[6 * pair * plane : 6 * pair * plane + depth, :]
        result = jnp.dot(band[1], window, preferred_element_type=jnp.float32)
        result = jnp.maximum(result + bias_ref[:, 2:3], 0.0).astype(jnp.bfloat16)
        for yo in range(2):
            for zo in range(Z):
                rows = (yo * Z + zo) * channels
                start = (2 * pair + yo) * channels
                third[zo, start : start + channels, :] = result[rows : rows + channels]
    size = YB * channels
    line = iota((size, size), 0)
    swap = onehot(iota((size, size), 1) == line % YB * channels + line // YB)
    for zo in range(Z):
        moved = jnp.dot(swap, third[zo], preferred_element_type=jnp.float32)
        out_ref[:, zo, :, :] = moved.reshape(channels, YB, third.shape[2]).astype(jnp.bfloat16)


def network(image, taps, band, biases, channels):
    width = image.shape[1]
    plane = Z * channels
    vmem = pl.BlockSpec(memory_space=pltpu.VMEM)
    hbm = pl.BlockSpec(memory_space=pltpu.HBM)
    inputs = (image, taps, band, biases)
    return pl.pallas_call(
        convolutions,
        out_shape=jax.ShapeDtypeStruct((channels, Z, YB, width), jnp.bfloat16),
        in_specs=[hbm] * 4,
        out_specs=vmem,
        scratch_shapes=[pltpu.VMEM(value.shape, value.dtype) for value in inputs]
        + [
            pltpu.VMEM((3 * plane * (YB + 4), width), jnp.bfloat16),
            pltpu.VMEM((3 * plane * (YB + 2), width), jnp.bfloat16),
            pltpu.VMEM((Z, YB * channels, width), jnp.bfloat16),
            pltpu.SemaphoreType.DMA((4,)),
        ],
        compiler_params=pltpu.CompilerParams(vmem_limit_bytes=VMEM_BYTES),
        name="network",
    )(*inputs)


def on_device(
    tiles,
    entry_dest,
    entry_tile,
    entry_z,
    entry_xb,
    entry_ky,
    entry_kx,
    wy_table,
    wx_table,
    w_first,
    b_first,
    w_second,
    b_second,
    w_third,
    b_third,
):
    prepared = rendered_window(
        tiles,
        (entry_dest, entry_tile, entry_z, entry_xb, entry_ky, entry_kx),
        wy_table,
        wx_table,
        (w_first, w_second, w_third),
        (b_first, b_second, b_third),
    )
    return network(*prepared, w_first.shape[0])


def solution(mesh):
    return jax.shard_map(
        on_device,
        mesh=mesh,
        in_specs=(
            P(("groups", "gy"), None, None),
            P("groups", None),
            P("groups"),
            P("groups"),
            P("groups"),
            P("groups"),
            P("groups"),
            P(),
            P(),
            P(),
            P(),
            P(),
            P(),
            P(),
            P(),
        ),
        out_specs=P(None, "groups", "gy", None),
        check_vma=False,
    )
```
